32 devices in a mesh: ctx: 8 (over z, y), head: 4 (over x, core).
Axes of the slice: x: 2, y: 2, z: 4, core: 2. Of those that a mesh axis runs over, the one named last changes fastest.
Arguments:
- queries: bfloat16 [2048, 12288], P(('ctx', 'head')), may hold values from -96 to 96
- key_rows: bfloat16 [2048, 768], P(('ctx', 'head')), may hold values from -8 to 8
- values: bfloat16 [2048, 512], P(('ctx', 'head')), may hold values from -6 to 6
- gate_logits: bfloat16 [2048, 128], P(('ctx', 'head')), may hold values from -6 to 6
- key_mix: bfloat16 [4, 32, 192], replicated, may hold values from -1 to 1
- key_proj: bfloat16 [4, 192, 192], replicated, may hold values from -1 to 1
- value_mix: bfloat16 [4, 32, 128], replicated, may hold values from -1 to 1
- value_proj: bfloat16 [4, 128, 128], replicated, may hold values from -0.5 to 0.5
Outputs:
- mixture: bfloat16 [2048, 8192], P(('ctx', 'head'))
The draws below stay inside these ranges and needn't reach their ends.
All inputs are finite; a program needn't handle non-finite values.
Results may differ from the reference program's by a relative error of at most 0.012.
Values may be sent and summed in bfloat16 or wider, within the bound.
No kernel may reach another device: no remote copies, remote signals or barrier semaphores. Data moves between devices by JAX's collectives and lax.ppermute only.
A program may use at most 64 MiB of HBM per device.

```python
import math
import jax
import jax.numpy as jnp
from jax import lax

QHEADS = 64
GROUPS = 4
KDIM = 192
VDIM = 128
BLOCK = 32
STRIDE = 16
WINDOW = 512
TOKENS = 2048
NBLOCKS = 128


def base_draws(key):
    key_first = jax.random.fold_in(key, 101)
    key_second = jax.random.fold_in(key, 102)
    key_third = jax.random.fold_in(key, 103)
    rows_raw = jax.random.normal(key_first, (TOKENS, GROUPS, KDIM), jnp.float32)
    mixer = jax.random.normal(key_second, (GROUPS, BLOCK, KDIM), jnp.float32) / math.sqrt(BLOCK)
    projection = jax.random.normal(key_third, (GROUPS, KDIM, KDIM), jnp.float32) / math.sqrt(KDIM)
    rows_out = jnp.clip(rows_raw, -8.0, 8.0).astype(jnp.bfloat16)
    mixer = jnp.clip(mixer, -1.0, 1.0).astype(jnp.bfloat16)
    projection = jnp.clip(projection, -1.0, 1.0).astype(jnp.bfloat16)
    return (rows_out, mixer, projection)


def draw_queries(key, part):
    key_base = jax.random.fold_in(key, 201)
    drawn = jax.random.normal(key_base, (TOKENS, QHEADS, KDIM), jnp.float32) * 2.0
    drawn = jnp.clip(drawn, -8.0, 8.0)
    return drawn.reshape(TOKENS, QHEADS * KDIM).astype(jnp.bfloat16)


def draw_key_rows(key, part):
    rows_key, mixer, projection = base_draws(key)
    return rows_key.reshape(TOKENS, GROUPS * KDIM)


def draw_key_mix(key, part):
    rows_key, mixer, projection = base_draws(key)
    return mixer


def draw_key_proj(key, part):
    rows_key, mixer, projection = base_draws(key)
    return projection


def block_levels(own_key, extent, shards, least, largest):
    level, own = 1.0, jax.random.fold_in(own_key, 6)
    for axis_at, parts in shards:
        steps = jnp.exp(jax.random.uniform(jax.random.fold_in(own, axis_at), (parts,), jnp.float32, least / len(shards), largest / len(shards)))
        level = level * jnp.repeat(steps, extent[axis_at] // parts).reshape([-1 if axis == axis_at else 1 for axis in range(len(extent))])
    return level


def gaussian(own_key, extent, scale, reach, shards=(), kind=jnp.bfloat16):
    values = scale * jax.random.normal(own_key, extent, jnp.float32)
    if shards:
        values = values * block_levels(own_key, extent, shards, -0.22, 0.18)
    return jnp.clip(values, -reach, reach).astype(kind)


def setup_inputs(seed: int = 0) -> dict:
    keys = jax.random.split(jax.random.key(seed), 9)
    return {
        "queries": draw_queries(jax.random.fold_in(keys[8], 71), 0),
        "key_rows": draw_key_rows(jax.random.fold_in(keys[8], 71), 0),
        "values": gaussian(keys[2], (TOKENS, GROUPS * VDIM), 1.0, 6.0, ((0, 32),)),
        "gate_logits": gaussian(keys[3], (TOKENS, 2 * QHEADS), 1.5, 6.0, ((0, 32),)),
        "key_mix": draw_key_mix(jax.random.fold_in(keys[8], 71), 0),
        "key_proj": draw_key_proj(jax.random.fold_in(keys[8], 71), 0),
        "value_mix": gaussian(keys[6], (GROUPS, BLOCK, VDIM), 0.177, 1.0),
        "value_proj": gaussian(keys[7], (GROUPS, VDIM, VDIM), VDIM ** -0.5, 0.5),
    }


def compress_rows(rows, mixer, projection):
    block_count = rows.shape[0] // STRIDE
    zero_rows = jnp.zeros((STRIDE, rows.shape[1], rows.shape[2]), jnp.float32)
    padded = jnp.concatenate([rows.astype(jnp.float32), zero_rows], 0)
    halves = padded.reshape(block_count + 1, STRIDE, rows.shape[1], rows.shape[2])
    weights = mixer.astype(jnp.float32)
    pooled = jnp.einsum('bjgd,gjd->bgd', halves[:-1], weights[:, :STRIDE], precision=lax.Precision.HIGHEST)
    pooled = pooled + jnp.einsum('bjgd,gjd->bgd', halves[1:], weights[:, STRIDE:], precision=lax.Precision.HIGHEST)
    pooled = lax.optimization_barrier(pooled.astype(jnp.bfloat16)).astype(jnp.float32)
    summary = jnp.einsum('bgd,gde->bge', pooled, projection.astype(jnp.float32), precision=lax.Precision.HIGHEST)
    return summary.astype(jnp.bfloat16)

def soft_mix(scores, visible, value_rows):
    masked = jnp.where(visible, scores, -1e+30)
    highest = lax.optimization_barrier(jnp.max(masked, axis=-1, keepdims=True))
    weights = jnp.where(visible, jnp.exp(scores - highest), 0.0)
    weight_total = lax.optimization_barrier(jnp.sum(weights, axis=-1))
    rounded = lax.optimization_barrier(weights.astype(jnp.bfloat16)).astype(jnp.float32)
    numerator = jnp.einsum('tghs,sgd->tghd', rounded, value_rows, precision=lax.Precision.HIGHEST)
    safe_total = jnp.where(weight_total > 0.0, weight_total, 1.0)
    return numerator / safe_total[..., None]

def reference(queries, key_rows, values, gate_logits, key_mix, key_proj, value_mix, value_proj):
    per_group = QHEADS // GROUPS
    score_scale = 1.0 / math.sqrt(KDIM)
    keys_all = key_rows.reshape(TOKENS, GROUPS, KDIM)
    values_all = values.reshape(TOKENS, GROUPS, VDIM)
    summary_keys = compress_rows(keys_all, key_mix, key_proj).astype(jnp.float32)
    summary_values = compress_rows(values_all, value_mix, value_proj).astype(jnp.float32)
    padded_keys = jnp.concatenate([jnp.zeros((WINDOW, GROUPS, KDIM), keys_all.dtype), keys_all], 0)
    padded_values = jnp.concatenate([jnp.zeros((WINDOW, GROUPS, VDIM), values_all.dtype), values_all], 0)
    query_block = math.gcd(512, TOKENS)
    block_ends = jnp.arange(NBLOCKS, dtype=jnp.int32) * STRIDE + BLOCK - 1

    def one_block(block_index):
        first = (block_index * query_block).astype(jnp.int32)
        query_part = lax.dynamic_slice_in_dim(queries, first, query_block, 0)
        query_part = query_part.reshape(query_block, GROUPS, per_group, KDIM).astype(jnp.float32)
        gate_part = lax.dynamic_slice_in_dim(gate_logits, first, query_block, 0)
        gate_values = jax.nn.sigmoid(gate_part.reshape(query_block, GROUPS, per_group, 2).astype(jnp.float32))
        positions = first + jnp.arange(query_block, dtype=jnp.int32)
        scores = jnp.einsum('tghd,bgd->tghb', query_part, summary_keys, precision=lax.Precision.HIGHEST) * score_scale
        visible = (block_ends[None, :] <= positions[:, None])[:, None, None, :]
        compressed_out = soft_mix(scores, visible, summary_values)
        near_keys = lax.dynamic_slice_in_dim(padded_keys, first, query_block + WINDOW, 0).astype(jnp.float32)
        near_values = lax.dynamic_slice_in_dim(padded_values, first, query_block + WINDOW, 0).astype(jnp.float32)
        key_places = first - WINDOW + jnp.arange(query_block + WINDOW, dtype=jnp.int32)
        near_visible = (key_places[None, :] <= positions[:, None]) & (key_places[None, :] > positions[:, None] - WINDOW) & (key_places[None, :] >= 0)
        scores = jnp.einsum('tghd,sgd->tghs', query_part, near_keys, precision=lax.Precision.HIGHEST) * score_scale
        window_out = soft_mix(scores, near_visible[:, None, None, :], near_values)
        mixture = gate_values[..., 0:1] * compressed_out + gate_values[..., 1:2] * window_out
        return mixture.astype(jnp.bfloat16).reshape(query_block, QHEADS * VDIM)
    blocks = lax.map(one_block, jnp.arange(TOKENS // query_block, dtype=jnp.int32))
    return blocks.reshape(TOKENS, QHEADS * VDIM)
```

```python
import functools
import math

import jax
import jax.numpy as jnp
from jax import lax
from jax.experimental import pallas as pl
from jax.experimental.pallas import tpu as pltpu
from jax.sharding import Mesh, PartitionSpec as P

QHEADS = 64
GROUPS = 4
PER_GROUP = QHEADS // GROUPS
KDIM = 192
VDIM = 128
BLOCK = 32
STRIDE = 16
WINDOW = 512
KCOLS = GROUPS * KDIM
VCOLS = GROUPS * VDIM
COLS = KCOLS + VCOLS
CROWS = 8
LOG2E = 1.4426950408889634
HIDE = -1e30
HEADS_AT_ONCE = 4
WIDE = 256
AXES = ("slab", "member")


def split_hi_lo(x):
    hi = x.astype(jnp.bfloat16).astype(jnp.float32)
    return hi, x - hi


def pooled_halves(rows, mix):
    halves = rows.shape[0] // STRIDE
    cut = rows.reshape(halves, STRIDE, rows.shape[1])
    first = jnp.sum(cut * mix[None, :STRIDE], axis=1)
    second = jnp.sum(cut * mix[None, STRIDE:], axis=1)
    return first, second


def compress_rows(rows, mix_ref, proj_ref, width):
    mix = jnp.concatenate([mix_ref[g].astype(jnp.float32) for g in range(GROUPS)], axis=1)
    first, second = pooled_halves(rows.astype(jnp.float32), mix)
    count = first.shape[0]
    whole = first[: count - 1] + second[1:]
    a_hi, a_lo = split_hi_lo(first[count - 1 :])
    b_hi, b_lo = split_hi_lo(second[:1])
    pad = jnp.zeros((CROWS - (count - 1) - 4, rows.shape[1]), jnp.float32)
    stacked = jnp.concatenate([whole, a_hi, a_lo, b_hi, b_lo, pad], axis=0)
    out = []
    for g in range(GROUPS):
        part = stacked[:, g * width : (g + 1) * width].astype(jnp.bfloat16)
        out.append(jnp.dot(part, proj_ref[g], preferred_element_type=jnp.float32))
    out = jnp.concatenate(out, axis=1)
    x_hi, x_lo = split_hi_lo(out[count - 1 : count] + out[count : count + 1])
    y_hi, y_lo = split_hi_lo(out[count + 1 : count + 2] + out[count + 2 : count + 3])
    return jnp.concatenate([out[: count - 1], x_hi, x_lo, y_hi, y_lo, pad], axis=0)


def pack_kernel(k_ref, v_ref, kmix_ref, kproj_ref, vmix_ref, vproj_ref, packed_ref, small_ref):
    rows = k_ref.shape[0]
    packed_ref[:rows, :KCOLS] = k_ref[...]
    packed_ref[:rows, KCOLS:] = v_ref[...]
    ck = compress_rows(k_ref[...], kmix_ref, kproj_ref, KDIM).astype(jnp.bfloat16)
    cv = compress_rows(v_ref[...], vmix_ref, vproj_ref, VDIM).astype(jnp.bfloat16)
    small_ref[:, :KCOLS] = ck
    small_ref[:, KCOLS:] = cv
    packed_ref[rows:, :KCOLS] = ck
    packed_ref[rows:, KCOLS:] = cv


def pack(keys, values, key_mix, key_proj, value_mix, value_proj):
    rows = keys.shape[0]
    return pl.pallas_call(
        pack_kernel,
        out_shape=(
            jax.ShapeDtypeStruct((rows + CROWS, COLS), jnp.bfloat16),
            jax.ShapeDtypeStruct((CROWS, COLS), jnp.bfloat16),
        ),
        name="pack",
    )(keys, values, key_mix, key_proj, value_mix, value_proj)


def attend_kernel(slabs, members, rows, place_ref, *refs):
    pairs = members // 2 - 1
    own_ref, before_ref, mixed_ref = refs[:3]
    near_refs = refs[3 : 3 + 2 * pairs]
    far_refs = refs[3 + 2 * pairs : 3 + 2 * pairs + slabs - 1]
    q_ref, gate_ref, out_ref, ke_ref, ko_ref, vt_ref, wbias_ref, cbias_ref, crow_ref = refs[
        3 + 2 * pairs + slabs - 1 :
    ]
    slab = place_ref[0]
    member = place_ref[1]
    device = slab * members + member
    nblocks = slabs * members * (rows // STRIDE)
    per = rows // STRIDE
    wkeys = (members + 1) * rows
    half = WIDE - KDIM

    @pl.when(pl.program_id(0) == 0)
    def _():
        lane = lax.broadcasted_iota(jnp.int32, (1, WIDE), 1)

        def place_keys(at, block):
            count = block.shape[0]
            for g in range(GROUPS):
                start = g * KDIM
                lead = start % 128
                piece = block[:, start - lead : start - lead + WIDE]
                if lead == 0:
                    even = jnp.where(lane < KDIM, piece, jnp.zeros_like(piece))
                    odd = jnp.concatenate([even[:, KDIM:], even[:, :KDIM]], axis=1)
                else:
                    odd = jnp.where(lane >= half, piece, jnp.zeros_like(piece))
                    even = jnp.concatenate([odd[:, half:], odd[:, :half]], axis=1)
                ke_ref[g, at : at + count, :] = even
                ko_ref[g, at : at + count, :] = odd

        key_row = lax.broadcasted_iota(jnp.int32, (rows, 2 * rows), 0)
        token = lax.broadcasted_iota(jnp.int32, (rows, 2 * rows), 1) % rows
        sources = [(own_ref, device), (before_ref, device - members)]
        odd_member = member % 2
        sources.append((mixed_ref, jnp.where(odd_member == 1, device - 1, device - members + 1)))
        chip = member // 2
        for index in range(pairs):
            k = 2 * (index + 1)
            for swapped in range(2):
                other = jnp.bitwise_xor(member, k + swapped)
                earlier = jnp.where(other // 2 < chip, slab, slab - 1)
                sources.append((near_refs[2 * index + swapped], earlier * members + other))
        value_parts = []
        for at, (ref, base) in enumerate(sources):
            block = ref[:rows, :]
            place_keys(at * rows, block[:, :KCOLS])
            value_parts.append(block[:, KCOLS:])
            distance = (device - base) * rows + token - key_row
            seen = (distance >= 0) & (distance < WINDOW) & (base >= 0)
            wbias_ref[at * rows : (at + 1) * rows, :] = jnp.where(seen, 0.0, HIDE)
        all_values = jnp.concatenate(value_parts, axis=0)

        def put_rows(at, block):
            block = block.astype(jnp.float32)
            for c in range(COLS // 128):
                crow_ref[c, pl.ds(at, CROWS), :] = block[:, c * 128 : (c + 1) * 128]

        put_rows(slabs * members * CROWS, jnp.zeros((CROWS, COLS), jnp.float32))
        for s in range(slabs):
            at_slab = jnp.bitwise_xor(slab, s)
            at = pl.multiple_of((at_slab * members + member) * CROWS, CROWS)
            if s == 0:
                row = own_ref[rows:, :]
            else:
                row = far_refs[s - 1][...]
            put_rows(at, row)
            for ref, flip in [(mixed_ref, 1)] + [
                (near_refs[2 * index + swapped], 2 * (index + 1) + swapped)
                for index in range(pairs)
                for swapped in range(2)
            ]:
                at = (at_slab * members + jnp.bitwise_xor(member, flip)) * CROWS
                at = pl.multiple_of(at, CROWS)
                row = ref[rows + s * CROWS : rows + (s + 1) * CROWS, :]
                put_rows(at, row)
        count = slabs * members

        def kind(r, shift=0):
            rows_of = pl.ds(r + shift * CROWS, count, stride=CROWS)
            return jnp.concatenate([crow_ref[c, rows_of, :] for c in range(COLS // 128)], axis=1)

        kinds = [kind(r) for r in range(per - 1)]
        kinds.append(kind(per - 1) + kind(per) + kind(per + 1, 1) + kind(per + 2, 1))
        crows = jnp.concatenate([x.astype(jnp.bfloat16) for x in kinds], axis=0)
        place_keys(wkeys, crows[:, :KCOLS])
        all_values = jnp.concatenate([all_values, crows[:, KCOLS:]], axis=0)
        for g in range(GROUPS):
            vt_ref[g, :VDIM, :] = all_values[:, g * VDIM : (g + 1) * VDIM].T
        vt_ref[:, VDIM:, :] = jnp.ones(
            (GROUPS, vt_ref.shape[1] - VDIM, vt_ref.shape[2]), jnp.bfloat16
        )
        at = lax.broadcasted_iota(jnp.int32, (nblocks, 2 * rows), 0)
        token = device * rows + lax.broadcasted_iota(jnp.int32, (nblocks, 2 * rows), 1) % rows
        block_index = (at % count) * per + at // count
        cbias_ref[...] = jnp.where(block_index * STRIDE + BLOCK - 1 <= token, 0.0, HIDE)

    g = pl.program_id(0)
    factor = LOG2E / math.sqrt(KDIM)
    lanes = HEADS_AT_ONCE * rows

    def branch(scores, bias, value_t):
        scores = scores + jnp.concatenate([bias] * (lanes // (2 * rows)), axis=1)
        highest = jnp.maximum(jnp.max(scores, axis=0, keepdims=True), -1e29)
        weights = jnp.exp2((scores - highest) * factor).astype(jnp.bfloat16)
        mixed = jnp.dot(value_t, weights, preferred_element_type=jnp.float32)
        total = mixed[VDIM : VDIM + 1]
        return mixed[:VDIM], jnp.where(total > 0.0, total, 1.0)

    for parity in range(2):
        keys_ref = ko_ref if parity else ke_ref
        for part in range(PER_GROUP // 2 // HEADS_AT_ONCE):
            q = []
            for u in range(HEADS_AT_ONCE):
                at = (part * HEADS_AT_ONCE + u) * 2 * KDIM + parity * (2 * KDIM - WIDE)
                q.append(q_ref[:, at : at + WIDE])
            q = jnp.concatenate(q, axis=0)
            scores = lax.dot_general(
                keys_ref[g], q, (((1,), (1,)), ((), ())), preferred_element_type=jnp.float32
            )
            near, near_total = branch(scores[:wkeys], wbias_ref[...], vt_ref[g, :, :wkeys])
            far, far_total = branch(scores[wkeys:], cbias_ref[...], vt_ref[g, :, wkeys:])
            row = 2 * (parity * (PER_GROUP // 2 // HEADS_AT_ONCE) + part)
            far_gate = gate_ref[0, row : row + 1, :] / far_total
            near_gate = gate_ref[0, row + 1 : row + 2, :] / near_total
            mixed = (far * far_gate + near * near_gate).T.astype(jnp.bfloat16)
            for u in range(HEADS_AT_ONCE):
                head = 2 * (part * HEADS_AT_ONCE + u) + parity
                out_ref[:, head * VDIM : (head + 1) * VDIM] = mixed[u * rows : (u + 1) * rows]


def attend(place, own, before, mixed, near, far, queries, gates, slabs, members):
    rows = queries.shape[0]
    count = slabs * members
    nblocks = count * (rows // STRIDE)
    keys = (members + 1) * rows + nblocks
    blocks = [own, before, mixed, *near, *far]
    whole = lambda x: pl.BlockSpec(x.shape, lambda g, *_: (0,) * x.ndim)
    return pl.pallas_call(
        functools.partial(attend_kernel, slabs, members, rows),
        grid_spec=pltpu.PrefetchScalarGridSpec(
            num_scalar_prefetch=1,
            grid=(GROUPS,),
            in_specs=[whole(x) for x in blocks]
            + [
                pl.BlockSpec((rows, PER_GROUP * KDIM), lambda g, *_: (0, g)),
                pl.BlockSpec((1,) + gates.shape[1:], lambda g, *_: (g, 0, 0)),
            ],
            out_specs=pl.BlockSpec((rows, PER_GROUP * VDIM), lambda g, *_: (0, g)),
            scratch_shapes=[
                pltpu.VMEM((GROUPS, keys, WIDE), jnp.bfloat16),
                pltpu.VMEM((GROUPS, keys, WIDE), jnp.bfloat16),
                pltpu.VMEM((GROUPS, VDIM + 16, keys), jnp.bfloat16),
                pltpu.VMEM(((members + 1) * rows, 2 * rows), jnp.float32),
                pltpu.VMEM((nblocks, 2 * rows), jnp.float32),
                pltpu.VMEM((COLS // 128, (count + 1) * CROWS, 128), jnp.float32),
            ],
        ),
        out_shape=jax.ShapeDtypeStruct((rows, QHEADS * VDIM), jnp.bfloat16),
        compiler_params=pltpu.CompilerParams(vmem_limit_bytes=60 << 20),
        name="attend",
    )(place, *blocks, queries, gates)


def local(slabs, members, queries, keys, values, gate_logits, key_mix, key_proj, value_mix, value_proj):
    rows = queries.shape[0]
    devices = slabs * members
    slab = lax.axis_index("slab")
    member = lax.axis_index("member")
    send = lambda x, pairs: lax.ppermute(x, AXES, pairs)
    flip = lambda k: [(d, d ^ k) for d in range(devices)]

    def across(d):
        low = d - members
        up = d + members
        if (d // members) % 2 == 1:
            return up if up < devices else d
        return low if low >= 0 else d

    packed, small = pack(keys, values, key_mix, key_proj, value_mix, value_proj)
    from_flip = send(packed, flip(members))
    from_odd = send(packed, [(d, across(d)) for d in range(devices)])
    if slabs <= 4:
        far = [from_flip[rows:]]
        far += [send(small, flip(members * s)) for s in range(2, slabs)]
    else:
        gathered = lax.all_gather(small, "slab", axis=0)
        far = [
            lax.dynamic_index_in_dim(gathered, slab ^ s, 0, keepdims=False) for s in range(1, slabs)
        ]
    before = jnp.where(slab % 2 == 1, from_flip[:rows], from_odd[:rows])
    own = packed[:rows]
    tail = jnp.concatenate([packed[rows:], *far], axis=0)
    bits = members.bit_length() - 1
    loads = [
        jnp.concatenate([jnp.where((member >> b) % 2 == 0, own, before), tail], axis=0)
        for b in range(bits)
    ]
    mixed = send(loads[0], flip(1))
    near = []
    for k in range(2, members, 2):
        got = send(loads[k.bit_length() - 1], flip(k))
        near += [got, send(got, flip(1))]
    parts = PER_GROUP // 2 // HEADS_AT_ONCE
    gates = jax.nn.sigmoid(gate_logits.astype(jnp.float32))
    gates = gates.reshape(rows, GROUPS, parts, HEADS_AT_ONCE, 2, 2).transpose(1, 4, 2, 5, 3, 0)
    gates = gates.reshape(GROUPS, 4 * parts, HEADS_AT_ONCE * rows)
    place = jnp.stack([slab, member]).astype(jnp.int32)
    return attend(place, packed, before, mixed, near, far, queries, gates, slabs, members)


def solution(mesh):
    devices = mesh.devices.size

    def whole(queries, *rest):
        rows = queries.shape[0] // devices
        members = WINDOW // rows
        slabs = devices // members
        assert members * rows == WINDOW and slabs * members == devices
        assert members & (members - 1) == 0 and slabs & (slabs - 1) == 0
        inner = Mesh(mesh.devices.reshape(slabs, members), AXES)
        split = P(AXES, None)
        step = jax.shard_map(
            functools.partial(local, slabs, members),
            mesh=inner,
            in_specs=(split, split, split, split, P(), P(), P(), P()),
            out_specs=split,
            check_vma=False,
        )
        return step(queries, *rest)

    return whole
```

```python
import functools
import math

import jax
import jax.numpy as jnp
from jax import lax
from jax.experimental import pallas as pl
from jax.experimental.pallas import tpu as pltpu
from jax.sharding import Mesh, PartitionSpec as P

QHEADS = 64
GROUPS = 4
PER_GROUP = QHEADS // GROUPS
KDIM = 192
VDIM = 128
BLOCK = 32
STRIDE = 16
WINDOW = 512
KCOLS = GROUPS * KDIM
VCOLS = GROUPS * VDIM
COLS = KCOLS + VCOLS
CROWS = 8
LOG2E = 1.4426950408889634
HIDE = -1e30
HEADS_AT_ONCE = 4
WIDE = 256
SUMS = 16
STATE = VDIM + SUMS
VMEM_GRANT = 40 << 20
VMEM_MOST = 63 << 20
AXES = ("slab", "member")
HALF = WIDE - KDIM
PARTS = PER_GROUP // 2 // HEADS_AT_ONCE
CHUNKS = 2 * PARTS
FACTOR = LOG2E / math.sqrt(KDIM)


def split_hi_lo(x):
    hi = x.astype(jnp.bfloat16).astype(jnp.float32)
    return hi, x - hi


def pooled_halves(rows, mix):
    halves = rows.shape[0] // STRIDE
    cut = rows.reshape(halves, STRIDE, rows.shape[1])
    first = jnp.sum(cut * mix[None, :STRIDE], axis=1)
    second = jnp.sum(cut * mix[None, STRIDE:], axis=1)
    return first, second


def compress_rows(rows, mix_ref, proj_ref, width):
    mix = jnp.concatenate([mix_ref[g].astype(jnp.float32) for g in range(GROUPS)], axis=1)
    first, second = pooled_halves(rows.astype(jnp.float32), mix)
    count = first.shape[0]
    whole = first[: count - 1] + second[1:]
    a_hi, a_lo = split_hi_lo(first[count - 1 :])
    b_hi, b_lo = split_hi_lo(second[:1])
    pad = jnp.zeros((CROWS - (count - 1) - 4, rows.shape[1]), jnp.float32)
    stacked = jnp.concatenate([whole, a_hi, a_lo, b_hi, b_lo, pad], axis=0)
    out = []
    for g in range(GROUPS):
        part = stacked[:, g * width : (g + 1) * width].astype(jnp.bfloat16)
        out.append(jnp.dot(part, proj_ref[g], preferred_element_type=jnp.float32))
    out = jnp.concatenate(out, axis=1)
    x_hi, x_lo = split_hi_lo(out[count - 1 : count] + out[count : count + 1])
    y_hi, y_lo = split_hi_lo(out[count + 1 : count + 2] + out[count + 2 : count + 3])
    return jnp.concatenate([out[: count - 1], x_hi, x_lo, y_hi, y_lo, pad], axis=0)


def pack_kernel(k_ref, v_ref, kmix_ref, kproj_ref, vmix_ref, vproj_ref, packed_ref, small_ref):
    rows = k_ref.shape[0]
    packed_ref[:rows, :KCOLS] = k_ref[...]
    packed_ref[:rows, KCOLS:] = v_ref[...]
    ck = compress_rows(k_ref[...], kmix_ref, kproj_ref, KDIM).astype(jnp.bfloat16)
    cv = compress_rows(v_ref[...], vmix_ref, vproj_ref, VDIM).astype(jnp.bfloat16)
    small_ref[:, :KCOLS] = ck
    small_ref[:, KCOLS:] = cv
    packed_ref[rows:, :KCOLS] = ck
    packed_ref[rows:, KCOLS:] = cv


def pack(keys, values, key_mix, key_proj, value_mix, value_proj):
    rows = keys.shape[0]
    return pl.pallas_call(
        pack_kernel,
        out_shape=(
            jax.ShapeDtypeStruct((rows + CROWS, COLS), jnp.bfloat16),
            jax.ShapeDtypeStruct((CROWS, COLS), jnp.bfloat16),
        ),
        name="pack",
    )(keys, values, key_mix, key_proj, value_mix, value_proj)


def load_kernel(slabs, members, own_ref, came_ref, *refs):
    rows = own_ref.shape[0] - CROWS
    far_refs = refs[: slabs - 2]
    out_refs = refs[slabs - 2 :]
    member = lax.axis_index("member")
    own = own_ref[:rows]
    before = came_ref[:rows]
    for bit, out_ref in enumerate(out_refs):
        high = (jnp.zeros((1, 1), jnp.int32) + member // 2**bit) % 2
        out_ref[:rows] = jnp.where(high == 0, own, before)
        out_ref[rows : rows + CROWS] = own_ref[rows:]
        out_ref[rows + CROWS : rows + 2 * CROWS] = came_ref[rows:]
        for index, far_ref in enumerate(far_refs):
            at = rows + (2 + index) * CROWS
            out_ref[at : at + CROWS] = far_ref[...]


def loads(own, came, far, slabs, members):
    rows = own.shape[0] - CROWS
    shape = jax.ShapeDtypeStruct((rows + slabs * CROWS, COLS), jnp.bfloat16)
    return pl.pallas_call(
        functools.partial(load_kernel, slabs, members),
        out_shape=(shape,) * (members.bit_length() - 1),
        name="loads",
    )(own, came, *far)


def fold_max(x):
    return jnp.max(x.reshape(x.shape[0] // 8, 8, x.shape[1]), axis=0)


def stage_kernel(slabs, members, rows, kinds, first, last, *refs):
    refs = list(refs)
    take = lambda count: [refs.pop(0) for _ in range(count)]
    (own_ref,) = take(1)
    source_refs = take(len(kinds))
    crow_sources = take(slabs - 1 + members - 1) if last else []
    q_ref, gate_ref = take(2)
    state_in_ref = None if first else take(1)[0]
    (out_ref,) = take(1)
    ke_ref, ko_ref, vt_ref, bias_ref, s_ref, p_ref = take(6)
    if last:
        crow_ref, cbias_ref, full_ref, sem = take(4)
    slab = lax.axis_index("slab")
    member = lax.axis_index("member")
    device = slab * members + member
    per = rows // STRIDE
    count = slabs * members
    nblocks = count * per
    wkeys = len(kinds) * rows
    keys = s_ref.shape[1]
    lanes = HEADS_AT_ONCE * rows
    lane = lax.broadcasted_iota(jnp.int32, (1, WIDE), 1)
    scalar = lambda x: jnp.zeros((1, 1), jnp.int32) + x

    def place_keys(at, block):
        size = block.shape[0]
        for g in range(GROUPS):
            start = g * KDIM
            lead = start % 128
            piece = block[:, start - lead : start - lead + WIDE]
            if lead == 0:
                even = jnp.where(lane < KDIM, piece, jnp.zeros_like(piece))
                odd = jnp.concatenate([even[:, KDIM:], even[:, :KDIM]], axis=1)
            else:
                odd = jnp.where(lane >= HALF, piece, jnp.zeros_like(piece))
                even = jnp.concatenate([odd[:, HALF:], odd[:, :HALF]], axis=1)
            ke_ref[g, at : at + size, :] = even
            ko_ref[g, at : at + size, :] = odd

    if first:
        key_row = lax.broadcasted_iota(jnp.int32, (rows, lanes), 0)
        token = lax.broadcasted_iota(jnp.int32, (rows, lanes), 1) % rows
        bias_ref[:rows, :] = jnp.where(key_row <= token, 0.0, HIDE)
        edge = (key_row > token) & (device >= members)
        bias_ref[rows:, :] = jnp.where(edge, 0.0, HIDE)
    stand_in = own_ref[:1, :]
    value_parts = []
    for at, (kind, ref) in enumerate(zip(kinds, source_refs)):
        block = ref[:rows, :]
        ones = jnp.ones((1, 1), jnp.bfloat16)
        shown, values = block[:, :KCOLS], block[:, KCOLS:]
        if kind not in ("own", "before"):
            if kind == "mixed":
                known = (scalar(member) % 2 == 1) | (scalar(slab) >= 1)
            else:
                known = (scalar(member ^ kind) // 2 < scalar(member) // 2) | (scalar(slab) >= 1)
            shown = jnp.where(known, shown, jnp.broadcast_to(stand_in[:, :KCOLS], shown.shape))
            values = jnp.where(known, values, jnp.zeros_like(values))
            ones = jnp.where(known, 1.0, 0.0).astype(jnp.bfloat16)
        place_keys(at * rows, shown)
        value_parts.append(values)
        ones = jnp.broadcast_to(ones, (SUMS, rows))
        for g in range(GROUPS):
            vt_ref[g, VDIM:, at * rows : (at + 1) * rows] = ones

    if last:

        def put_rows(at, block):
            block = block.astype(jnp.float32)
            for c in range(COLS // 128):
                crow_ref[c, pl.ds(at, CROWS), :] = block[:, c * 128 : (c + 1) * 128]

        put_rows(count * CROWS, jnp.zeros((CROWS, COLS), jnp.float32))
        for s in range(slabs):
            at_slab = jnp.where(slab >= s, slab - s, slab - s + slabs)
            if s == 0:
                row = own_ref[rows:, :]
            elif s == 1:
                row = crow_sources[0][rows:, :]
            else:
                row = crow_sources[s - 1][...]
            at = (at_slab * members + member) * CROWS
            put_rows(pl.multiple_of(at, CROWS), row)
            for flip in range(1, members):
                ref = crow_sources[slabs - 1 + flip - 1]
                at = (at_slab * members + jnp.bitwise_xor(member, flip)) * CROWS
                row = ref[rows + s * CROWS : rows + (s + 1) * CROWS, :]
                put_rows(pl.multiple_of(at, CROWS), row)

        def kind_rows(r, shift=0):
            at = pl.ds(r + shift * CROWS, count, stride=CROWS)
            return jnp.concatenate([crow_ref[c, at, :] for c in range(COLS // 128)], axis=1)

        crows = [kind_rows(r) for r in range(per - 1)]
        crows.append(
            kind_rows(per - 1) + kind_rows(per) + kind_rows(per + 1, 1) + kind_rows(per + 2, 1)
        )
        crows = jnp.concatenate([x.astype(jnp.bfloat16) for x in crows], axis=0)
        place_keys(wkeys, crows[:, :KCOLS])
        value_parts.append(crows[:, KCOLS:])
        vt_ref[:, VDIM:, wkeys:] = jnp.ones((GROUPS, SUMS, nblocks), jnp.bfloat16)
        at = lax.broadcasted_iota(jnp.int32, (nblocks, lanes), 0)
        token = device * rows + lax.broadcasted_iota(jnp.int32, (nblocks, lanes), 1) % rows
        block_index = (at % count) * per + at // count
        cbias_ref[...] = jnp.where(block_index * STRIDE + BLOCK - 1 <= token, 0.0, HIDE)

    all_values = jnp.concatenate(value_parts, axis=0)
    for g in range(GROUPS):
        vt_ref[g, :VDIM, :] = all_values[:, g * VDIM : (g + 1) * VDIM].T

    chunks = [(g, par, part) for g in range(GROUPS) for par in range(2) for part in range(PARTS)]

    def score(index, slot):
        g, parity, part = chunks[index]
        q = []
        for u in range(HEADS_AT_ONCE):
            at = g * PER_GROUP * KDIM
            at += (part * HEADS_AT_ONCE + u) * 2 * KDIM + parity * (2 * KDIM - WIDE)
            q.append(q_ref[:, at : at + WIDE])
        q = jnp.concatenate(q, axis=0)
        s = lax.dot_general(
            (ko_ref if parity else ke_ref)[g],
            q,
            (((1,), (1,)), ((), ())),
            preferred_element_type=jnp.float32,
        )
        near = s[:wkeys]
        if first:
            edge = near[: 2 * rows] + bias_ref[...]
            near = jnp.concatenate([edge, near[2 * rows :]], axis=0)
        s_ref[slot, :wkeys] = near
        near_max = jnp.max(fold_max(near), axis=0, keepdims=True)
        if not first:
            near_max = jnp.maximum(near_max, state_in_ref[index, VDIM + 1 : VDIM + 2])
        if not last:
            return (near_max,)
        far = s[wkeys:] + cbias_ref[...]
        s_ref[slot, wkeys:] = far
        return near_max, jnp.maximum(jnp.max(fold_max(far), axis=0, keepdims=True), -1e29)

    def weigh(slot, highest):
        for top, (start, stop) in zip(highest, ((0, wkeys), (wkeys, keys))):
            for at in range(start, stop, rows):
                w = jnp.exp2((s_ref[slot, at : at + rows] - top) * FACTOR)
                p_ref[slot, at : at + rows] = w.astype(jnp.bfloat16)

    def combine(index, slot, highest):
        g, parity, part = chunks[index]

        def mix(start, stop):
            return jnp.dot(
                vt_ref[g, :, start:stop],
                p_ref[slot, start:stop],
                preferred_element_type=jnp.float32,
            )

        near = mix(0, wkeys)
        if not first:
            scale = jnp.exp2((state_in_ref[index, VDIM + 1 : VDIM + 2] - highest[0]) * FACTOR)
            near_total = near[VDIM : VDIM + 1] + state_in_ref[index, VDIM : VDIM + 1] * scale
            near = near[:VDIM] + state_in_ref[index, :VDIM] * scale
        else:
            near_total = near[VDIM : VDIM + 1]
            near = near[:VDIM]
        if not last:
            out_ref[index, :VDIM] = near
            out_ref[index, VDIM : VDIM + 1] = near_total
            out_ref[index, VDIM + 1 : VDIM + 2] = highest[0]
            return
        far = mix(wkeys, keys)
        far_total = far[VDIM : VDIM + 1]
        far_total = jnp.where(far_total > 0.0, far_total, 1.0)
        row = 2 * index
        far_gate = gate_ref[row : row + 1, :] / far_total
        near_gate = gate_ref[row + 1 : row + 2, :] / near_total
        mixed = (far[:VDIM] * far_gate + near * near_gate).T.astype(jnp.bfloat16)
        for u in range(HEADS_AT_ONCE):
            head = g * PER_GROUP + 2 * (part * HEADS_AT_ONCE + u) + parity
            full_ref[:, head * VDIM : (head + 1) * VDIM] = mixed[u * rows : (u + 1) * rows]

    copies = []
    highest = score(0, 0)
    for index in range(len(chunks)):
        slot = index % 2
        if index + 1 < len(chunks):
            following = score(index + 1, 1 - slot)
        weigh(slot, highest)
        combine(index, slot, highest)
        highest = following
        if last and (index + 1) % CHUNKS == 0:
            g = index // CHUNKS
            width = PER_GROUP * VDIM
            copies.append(
                pltpu.make_async_copy(
                    full_ref.at[:, g * width : (g + 1) * width],
                    out_ref.at[:, g * width : (g + 1) * width],
                    sem.at[g],
                )
            )
            copies[-1].start()
    for copy in copies:
        copy.wait()


def stage(own, kinds, sources, crow_sources, queries, gates, state, slabs, members):
    rows = queries.shape[0]
    first = state is None
    last = crow_sources is not None
    count = slabs * members
    nblocks = count * (rows // STRIDE)
    keys = len(kinds) * rows + (nblocks if last else 0)
    lanes = HEADS_AT_ONCE * rows
    inputs = [own, *sources, *(crow_sources or []), queries, gates]
    if not first:
        inputs.append(state)
    scratch = [
        pltpu.VMEM((GROUPS, keys, WIDE), jnp.bfloat16),
        pltpu.VMEM((GROUPS, keys, WIDE), jnp.bfloat16),
        pltpu.VMEM((GROUPS, STATE, keys), jnp.bfloat16),
        pltpu.VMEM((2 * rows, lanes), jnp.float32),
        pltpu.VMEM((2, keys, lanes), jnp.float32),
        pltpu.VMEM((2, keys, lanes), jnp.bfloat16),
    ]
    if last:
        scratch += [
            pltpu.VMEM((COLS // 128, (count + 1) * CROWS, 128), jnp.float32),
            pltpu.VMEM((nblocks, lanes), jnp.float32),
            pltpu.VMEM((rows, QHEADS * VDIM), jnp.bfloat16),
            pltpu.SemaphoreType.DMA((GROUPS,)),
        ]
        out_shape = jax.ShapeDtypeStruct((rows, QHEADS * VDIM), jnp.bfloat16)
        out_spec = pl.BlockSpec(memory_space=pl.ANY)
    else:
        out_shape = jax.ShapeDtypeStruct((GROUPS * CHUNKS, VDIM + 8, lanes), jnp.float32)
        out_spec = pl.BlockSpec(memory_space=pltpu.VMEM)
    work = GROUPS * CHUNKS * lanes * keys
    return pl.pallas_call(
        functools.partial(stage_kernel, slabs, members, rows, kinds, first, last),
        out_shape=out_shape,
        in_specs=[pl.BlockSpec(memory_space=pltpu.VMEM)] * len(inputs),
        out_specs=out_spec,
        scratch_shapes=scratch,
        compiler_params=pltpu.CompilerParams(vmem_limit_bytes=VMEM_GRANT if slabs <= 4 else VMEM_MOST),
        cost_estimate=pl.CostEstimate(
            flops=2 * work * (WIDE + STATE), bytes_accessed=4 << 20, transcendentals=work
        ),
        name="stage_last" if last else "stage_first" if first else "stage_mid",
    )(*inputs)


def local(slabs, members, queries, keys, values, gate_logits, key_mix, key_proj, value_mix, value_proj):
    rows = queries.shape[0]
    devices = slabs * members
    send = lambda x, pairs: lax.ppermute(x, AXES, pairs)
    flip = lambda k: [(d, d ^ k) for d in range(devices)]
    onward = lambda k: [(d, d + k) for d in range(devices - k)]

    packed, small = pack(keys, values, key_mix, key_proj, value_mix, value_proj)
    came = send(packed, onward(members))
    if slabs <= 4:
        far = [send(small, onward(members * s)) for s in range(2, slabs)]
    else:
        slab = lax.axis_index("slab")
        gathered = lax.all_gather(small, "slab", axis=0)
        pick = lambda s: lax.dynamic_index_in_dim(gathered, (slab - s) % slabs, 0, keepdims=False)
        far = [pick(s) for s in range(2, slabs)]
    load = loads(packed, came, far, slabs, members)
    mixed = send(load[0], flip(1))
    near = {}
    for k in reversed(range(2, members, 2)):
        near[k] = send(load[k.bit_length() - 1], flip(k))
    for k in reversed(range(2, members, 2)):
        near[k + 1] = send(near[k], flip(1))
    gates = jax.nn.sigmoid(gate_logits.astype(jnp.float32))
    gates = gates.reshape(rows, GROUPS, PARTS, HEADS_AT_ONCE, 2, 2).transpose(1, 4, 2, 5, 3, 0)
    gates = gates.reshape(GROUPS * CHUNKS * 2, HEADS_AT_ONCE * rows)
    state = stage(
        packed,
        ("own", "before", "mixed"),
        [packed, came, mixed],
        None,
        queries,
        gates,
        None,
        slabs,
        members,
    )
    late = [kind for k in reversed(range(2, members, 2)) for kind in (k, k + 1)]
    crow_sources = [came, *far, mixed, *(near[k] for k in range(2, members))]
    return stage(
        packed,
        tuple(late),
        [near[k] for k in late],
        crow_sources,
        queries,
        gates,
        state,
        slabs,
        members,
    )


def solution(mesh):
    devices = mesh.devices.size

    def whole(queries, *rest):
        rows = queries.shape[0] // devices
        members = WINDOW // rows
        slabs = devices // members
        assert members * rows == WINDOW and slabs * members == devices
        assert members & (members - 1) == 0 and slabs & (slabs - 1) == 0
        inner = Mesh(mesh.devices.reshape(slabs, members), AXES)
        split = P(AXES, None)
        step = jax.shard_map(
            functools.partial(local, slabs, members),
            mesh=inner,
            in_specs=(split, split, split, split, P(), P(), P(), P()),
            out_specs=split,
            check_vma=False,
        )
        return step(queries, *rest)

    return whole
```
